32 devices in a mesh: seq: 8 (over y, x, core), cb: 4 (over z).
Axes of the slice: x: 2, y: 2, z: 4, core: 2. Of those that a mesh axis runs over, the one named last changes fastest.
Arguments:
- hidden: bfloat16 [2, 1024, 4096], P(None, 'seq'), may hold values from -6 to 6
- temporal_gain: float32 [4096], replicated, may hold values from 0.5 to 2
- temporal_qkv: bfloat16 [3, 4096, 2048], P(None, None, 'cb'), may hold values from -10 to 10
- temporal_out: bfloat16 [2048, 4096], P('cb'), may hold values from -0.125 to 0.125
- codebook_ids: int32 [2, 1024, 4], P(None, 'seq', 'cb'), may hold values from 0 to 2047
- embedding: bfloat16 [4, 2048, 1024], P('cb'), may hold values from -6 to 6
- input_weight: bfloat16 [4, 4096, 1024], P('cb', 'seq'), may hold values from -0.09375 to 0.09375
- depth_gain: float32 [4, 1024], P('cb'), may hold values from 0.5 to 2
- depth_qkv: bfloat16 [4, 3, 1024, 1024], P('cb'), may hold values from -10 to 10
- depth_out: bfloat16 [4, 1024, 1024], P('cb'), may hold values from -0.1875 to 0.1875
Outputs:
- temporal: bfloat16 [2, 1024, 4096], P(None, 'seq')
- depth: bfloat16 [2, 1024, 4, 1024], P(None, 'seq', 'cb')
The draws below stay inside these ranges and needn't reach their ends.
All inputs are finite; a program needn't handle non-finite values.
Results may differ from the reference program's by a relative error of at most 0.017.
Values may be sent and summed in bfloat16 or wider, within the bound.
No kernel may reach another device: no remote copies, remote signals or barrier semaphores. Data moves between devices by JAX's collectives and lax.ppermute only.
A program may use at most 128 MiB of HBM per device.

```python
import math
import jax
import jax.numpy as jnp
import numpy as np
from jax import lax

D = 4096
HEADS = 16
HD = 128
DW = 1024
DH = 16
DHD = 64
VOCAB = 2048
SEQS = 2
LEN = 1024
CODEBOOKS = 4
N_CB = 4


def shared_projection(key, width, head_count, head_size):
    first = jax.random.fold_in(key, 0)
    base = jnp.clip(jax.random.normal(first, (3, width, head_count * head_size), jnp.float32), -6.0, 6.0) / jnp.sqrt(jnp.float32(width))
    return base


def draw_temporal_qkv(key, part):
    return shared_projection(jax.random.fold_in(key, 11), D, HEADS, HD).astype(jnp.bfloat16)


def draw_depth_qkv(key, part):
    books = jax.random.split(jax.random.fold_in(key, 23), CODEBOOKS)
    stacked = jax.vmap(lambda book_key: shared_projection(book_key, DW, DH, DHD))(books)
    return stacked.astype(jnp.bfloat16)


def touch_ends(values, stream_key, least, largest):
    index_at = [jax.random.randint(jax.random.fold_in(stream_key, axis), (), 0, length) for axis, length in enumerate(values.shape)]
    widest = values.shape.index(max(values.shape))
    next_to = index_at[:widest] + [(index_at[widest] + 1) % values.shape[widest]] + index_at[widest + 1:]
    return values.at[tuple(index_at)].set(least).at[tuple(next_to)].set(largest)


def level_of(key, dims, cuts, smallest, high):
    loudness, own = 1.0, jax.random.fold_in(key, 6)
    for position, shards_of in cuts:
        steps = jnp.exp(jax.random.uniform(jax.random.fold_in(own, position), (shards_of,), jnp.float32, smallest / len(cuts), high / len(cuts)))
        loudness = loudness * jnp.repeat(steps, dims[position] // shards_of).reshape([-1 if axis == position else 1 for axis in range(len(dims))])
    return loudness


def rank_table(count, skew):
    loads = [(1 << 20) // math.isqrt(grade ** skew) + 1 for grade in range(1, count + 1)]
    deviation = 1 + sum(loads) // (1 << 30)
    return np.cumsum(np.array([max(1, weight // deviation) for weight in loads]))


def skewed_ids(own_key, dims, number_of, slope):
    table = rank_table(number_of, slope)
    ticket = jax.random.randint(jax.random.fold_in(own_key, 1), dims, 0, int(table[number_of - 1]))
    standing = jnp.searchsorted(jnp.asarray(table, jnp.int32), ticket, side="right")
    return jax.random.permutation(jax.random.fold_in(own_key, 2), number_of)[standing].astype(jnp.int32)


def normal_values(key, extent, deviation, bound, shards=(), kind=jnp.bfloat16):
    drawn = jax.random.normal(key, extent, jnp.float32) * deviation
    if len(shards) > 0:
        drawn = level_of(key, extent, shards, -0.22, 0.18) * drawn
    return jnp.clip(drawn, min=-bound, max=bound).astype(kind)


def setup_inputs(seed: int = 0) -> dict:
    key_list = jax.random.split(jax.random.key(seed), 11)
    return {
        "hidden": normal_values(key_list[0], (SEQS, LEN, D), 1.0, 6.0, ((1, 8),)),
        "temporal_gain": jnp.clip(jnp.exp(jax.random.uniform(key_list[1], (D,), jnp.float32, math.log(0.5), math.log(2.0))), 0.5, 2.0),
        "temporal_qkv": draw_temporal_qkv(jax.random.fold_in(key_list[10], 71), 0),
        "temporal_out": normal_values(key_list[3], (HEADS * HD, D), (HEADS * HD) ** -0.5, 0.125, ((0, 4),)),
        "codebook_ids": touch_ends(skewed_ids(key_list[4], (SEQS, LEN, CODEBOOKS), VOCAB, 2), jax.random.fold_in(key_list[4], 3), 0, VOCAB - 1).astype(jnp.int32),
        "embedding": normal_values(key_list[5], (CODEBOOKS, VOCAB, DW), 1.0, 6.0, ((0, 4),)),
        "input_weight": normal_values(key_list[6], (CODEBOOKS, D, DW), D ** -0.5, 0.09375, ((0, 4), (1, 8))),
        "depth_gain": jnp.clip(jnp.exp(math.log(2.0) - 1.3862944 * jax.random.uniform(key_list[7], (CODEBOOKS, DW), jnp.float32) ** level_of(key_list[7], (CODEBOOKS, DW), ((0, 4),), -0.2, 0.2)), 0.5, 2.0),
        "depth_qkv": draw_depth_qkv(jax.random.fold_in(key_list[10], 71), 0),
        "depth_out": normal_values(key_list[9], (CODEBOOKS, DW, DW), DW ** -0.5, 0.1875, ((0, 4),)),
    }


def normalize(values, scale):
    mean_sq = lax.optimization_barrier(jnp.mean(values * values, axis=-1, keepdims=True))
    return values * lax.rsqrt(mean_sq + 1e-05) * scale

def rounded(values):
    return lax.optimization_barrier(values.astype(jnp.bfloat16)).astype(jnp.float32)

def reference(hidden, temporal_gain, temporal_qkv, temporal_out, codebook_ids, embedding, input_weight, depth_gain, depth_qkv, depth_out):
    row_count = SEQS * LEN
    hidden_f = hidden.astype(jnp.float32)
    normed = normalize(hidden_f, temporal_gain).astype(jnp.bfloat16).reshape(row_count, D)
    projected = []
    for which in range(3):
        part_rows = jnp.dot(normed, temporal_qkv[which], preferred_element_type=jnp.float32).astype(jnp.bfloat16)
        projected.append(part_rows.reshape(SEQS, LEN, HEADS, HD).transpose(2, 0, 1, 3))
    positions = jnp.arange(LEN, dtype=jnp.int32)
    allowed = positions[:, None] >= positions[None, :]

    def one_head(operands):
        head_query, head_key, head_value = operands
        scores = jnp.einsum('sqd,skd->sqk', head_query.astype(jnp.float32), head_key.astype(jnp.float32)) / jnp.sqrt(jnp.float32(HD))
        scores = jnp.where(allowed[None], scores, -1e+30)
        highest = lax.optimization_barrier(jnp.max(scores, axis=-1, keepdims=True))
        weights = jnp.where(allowed[None], jnp.exp(scores - highest), 0.0)
        totals = lax.optimization_barrier(jnp.sum(weights, axis=-1, keepdims=True))
        mixed = jnp.einsum('sqk,skd->sqd', rounded(weights), head_value.astype(jnp.float32)) / totals
        return mixed.astype(jnp.bfloat16)
    mixed = lax.map(one_head, (projected[0], projected[1], projected[2]))
    mixed = mixed.transpose(1, 2, 0, 3).reshape(row_count, HEADS * HD)
    group_cols = HEADS * HD // N_CB
    summed = jnp.zeros((row_count, D), jnp.float32)
    for group_at in range(N_CB):
        term = jnp.dot(mixed[:, group_at * group_cols:(group_at + 1) * group_cols], temporal_out[group_at * group_cols:(group_at + 1) * group_cols], preferred_element_type=jnp.float32)
        summed = summed + rounded(term)
    temporal = (hidden_f.reshape(row_count, D) + summed).astype(jnp.bfloat16)
    id_rows = codebook_ids.reshape(row_count, CODEBOOKS).transpose(1, 0)

    def prepare(operands):
        in_weight, table, gain_row, qkv_weight, id_row = operands
        entry = jnp.take(table, id_row, axis=0).astype(jnp.float32)
        stream = (jnp.dot(temporal, in_weight, preferred_element_type=jnp.float32) + entry).astype(jnp.bfloat16)
        depth_normed = normalize(stream.astype(jnp.float32), gain_row).astype(jnp.bfloat16)
        book_query = jnp.dot(depth_normed, qkv_weight[0], preferred_element_type=jnp.float32).astype(jnp.bfloat16)
        book_key = jnp.dot(depth_normed, qkv_weight[1], preferred_element_type=jnp.float32).astype(jnp.bfloat16)
        book_value = jnp.dot(depth_normed, qkv_weight[2], preferred_element_type=jnp.float32).astype(jnp.bfloat16)
        return (stream, book_query, book_key, book_value)
    streams, queries, key_all, value_all = lax.map(prepare, (input_weight, embedding, depth_gain, depth_qkv, id_rows))
    key_heads = key_all.reshape(CODEBOOKS, row_count, DH, DHD)
    value_heads = value_all.reshape(CODEBOOKS, row_count, DH, DHD)
    book_numbers = jnp.arange(CODEBOOKS, dtype=jnp.int32)

    def attend(operands):
        book, query_rows, out_weight, stream_rows = operands
        query_heads = query_rows.reshape(row_count, DH, DHD).astype(jnp.float32)
        scores = jnp.einsum('rhd,jrhd->rhj', query_heads, key_heads.astype(jnp.float32)) / jnp.sqrt(jnp.float32(DHD))
        permitted = (book_numbers <= book)[None, None, :]
        scores = jnp.where(permitted, scores, -1e+30)
        highest = lax.optimization_barrier(jnp.max(scores, axis=-1, keepdims=True))
        weights = jnp.where(permitted, jnp.exp(scores - highest), 0.0)
        totals = lax.optimization_barrier(jnp.sum(weights, axis=-1))[..., None]
        book_mixed = jnp.einsum('rhj,jrhd->rhd', rounded(weights), value_heads.astype(jnp.float32)) / totals
        book_mixed = book_mixed.astype(jnp.bfloat16).reshape(row_count, DW)
        return (jnp.dot(book_mixed, out_weight, preferred_element_type=jnp.float32) + stream_rows.astype(jnp.float32)).astype(jnp.bfloat16)
    depth = lax.map(attend, (book_numbers, queries, depth_out, streams))
    depth = depth.transpose(1, 0, 2).reshape(SEQS, LEN, CODEBOOKS, DW)
    return (temporal.reshape(SEQS, LEN, D), depth)
```

```python
import functools

import jax
import jax.numpy as jnp
from jax import lax
from jax.experimental import pallas as pl
from jax.experimental.pallas import tpu as pltpu
from jax.sharding import PartitionSpec as P

HD = 128
DHD = 64
EPS = 1e-05
NEG = -1e30
F32 = jnp.float32
BF16 = jnp.bfloat16
CHUNKS = 2
VMEM_LIMIT = 60 * 1024 * 1024


VM = pl.BlockSpec(memory_space=pltpu.VMEM)
SM = pl.BlockSpec(memory_space=pltpu.SMEM)
ANY = pl.BlockSpec(memory_space=pl.ANY)
PARAMS = pltpu.CompilerParams(vmem_limit_bytes=VMEM_LIMIT)


def cost(flops, moved):
    return pl.CostEstimate(flops=flops, bytes_accessed=moved, transcendentals=0)


def dot(a, b):
    return jnp.dot(a, b, preferred_element_type=F32)


def flip(x, axis, bit):
    return lax.ppermute(x, axis, [(i, i ^ bit) for i in range(lax.axis_size(axis))])


def shift(x, axis, by):
    size = lax.axis_size(axis)
    return lax.ppermute(x, axis, [(i, (i + by) % size) for i in range(size)])


def spread(piece, axis, order):
    held = {0: piece}
    for bit in order:
        held.update({at ^ bit: flip(value, axis, bit) for at, value in list(held.items())})
    held.update({at ^ 1: flip(value, axis, 1) for at, value in list(held.items())})
    return held


def spread_halves(first, second, axis):
    size = lax.axis_size(axis)
    bits = [1 << place for place in range(1, size.bit_length() - 1)]
    a = spread(first, axis, bits)
    b = spread(second, axis, bits[::-1])
    return [half for at in range(size) for half in (a[at], b[at])]


def project_body(hidden_ref, gain_ref, weight_ref, out_ref, normed_ref):
    seqs, heads, frames, _ = out_ref.shape
    rows = normed_ref.shape[0]
    step = min(64, rows)

    @pl.when(pl.program_id(0) == 0)
    def _():
        def one(at, carry):
            span = pl.ds(pl.multiple_of(at * step, step), step)
            values = hidden_ref[span, :].astype(F32)
            mean_sq = jnp.mean(values * values, axis=-1, keepdims=True)
            normed_ref[span, :] = (values * lax.rsqrt(mean_sq + EPS) * gain_ref[...]).astype(BF16)
            return carry

        lax.fori_loop(0, rows // step, one, 0)

    result = dot(normed_ref[...], weight_ref[0]).astype(BF16)
    for s in range(seqs):
        for h in range(heads):
            out_ref[s, h] = result[s * frames : (s + 1) * frames, h * HD : (h + 1) * HD]


def project(hidden, gain, weight):
    seqs, frames, width = hidden.shape
    cols = weight.shape[2]
    heads = cols // HD
    per = min(2, heads)
    parts = heads // per
    rows = seqs * frames
    return pl.pallas_call(
        project_body,
        grid=(3 * parts,),
        in_specs=[
            pl.BlockSpec((rows, width), lambda i: (0, 0)),
            pl.BlockSpec((1, width), lambda i: (0, 0)),
            pl.BlockSpec((1, width, per * HD), lambda i: (i // parts, 0, i % parts)),
        ],
        out_specs=pl.BlockSpec((seqs, per, frames, HD), lambda i: (0, i % parts, 0, i // parts)),
        out_shape=jax.ShapeDtypeStruct((seqs, heads, frames, 3 * HD), BF16),
        scratch_shapes=[pltpu.VMEM((rows, width), BF16)],
        compiler_params=PARAMS,
        cost_estimate=cost(6 * rows * width * cols, 6 * width * cols + 2 * rows * width),
    )(hidden.reshape(rows, width), gain.reshape(1, width), weight)


def attend_body(packed_ref, out_ref):
    length = packed_ref.shape[0]
    block = min(256, length)
    scale = 1.0 / (HD**0.5)
    for start in range(0, length, block):
        stop = start + block
        scores = (
            lax.dot_general(
                packed_ref[start:stop, :HD],
                packed_ref[:stop, HD : 2 * HD],
                (((1,), (1,)), ((), ())),
                preferred_element_type=F32,
            )
            * scale
        )
        rows = lax.broadcasted_iota(jnp.int32, scores.shape, 0) + start
        cols = lax.broadcasted_iota(jnp.int32, scores.shape, 1)
        scores = jnp.where(cols <= rows, scores, NEG)
        weights = jnp.exp(scores - jnp.max(scores, axis=-1, keepdims=True))
        totals = jnp.sum(weights, axis=-1, keepdims=True)
        mixed = dot(weights.astype(BF16), packed_ref[:stop, 2 * HD :])
        out_ref[start:stop, :] = (mixed / totals).astype(BF16)


def attend_pair(packed):
    length = packed.shape[0]
    return pl.pallas_call(
        attend_body,
        in_specs=[VM],
        out_specs=VM,
        out_shape=jax.ShapeDtypeStruct((length, HD), BF16),
        compiler_params=PARAMS,
        cost_estimate=cost(3 * length * length * HD, 8 * length * HD),
    )(packed)


def temporal_attention(packed):
    seqs, heads, frames, _ = packed.shape
    pairs = seqs * heads
    size = lax.axis_size("seq")
    if pairs == size:
        whole = lax.all_to_all(
            packed.reshape(pairs, frames, 3 * HD), "seq", split_axis=0, concat_axis=0, tiled=True
        )
        mixed = attend_pair(whole.reshape(size * frames, 3 * HD))
        return lax.all_to_all(
            mixed.reshape(size, frames, HD), "seq", split_axis=0, concat_axis=0, tiled=True
        )
    queries = packed[..., :HD]
    both = lax.all_gather(packed[..., HD:], "seq", axis=2, tiled=True)
    keys, values = both[..., :HD], both[..., HD:]
    scores = jnp.einsum("shqd,shkd->shqk", queries, keys, preferred_element_type=F32) / (HD**0.5)
    at = lax.axis_index("seq") * frames + jnp.arange(frames, dtype=jnp.int32)
    allowed = jnp.arange(size * frames, dtype=jnp.int32)[None, :] <= at[:, None]
    scores = jnp.where(allowed, scores, NEG)
    weights = jnp.exp(scores - jnp.max(scores, axis=-1, keepdims=True))
    totals = jnp.sum(weights, axis=-1, keepdims=True)
    mixed = jnp.einsum(
        "shqk,shkd->shqd", weights.astype(BF16), values, preferred_element_type=F32
    )
    return (mixed / totals).astype(BF16).reshape(pairs, frames, HD)


def output_body(place_ref, hidden_ref, *refs):
    books = place_ref.shape[0] - 2
    del books
    mixed_refs, (own_ref,), pieces, (out_ref, cat_ref, weight_ref, sems) = refs
    size, groups, _, half, block = weight_ref.shape
    seqs_heads, frames, _ = mixed_refs[0].shape
    cols = 2 * half
    heads = cols // HD
    me = place_ref[0]

    def copies(at):
        column = pl.multiple_of((me ^ at) * block, block)
        found = []
        for side in range(2):
            found.append(
                pltpu.make_async_copy(
                    own_ref.at[side * half : (side + 1) * half, pl.ds(column, block)],
                    weight_ref.at[at, 0, side],
                    sems.at[at, side],
                )
            )
            found.append(
                pltpu.make_async_copy(
                    pieces[2 * at + side], weight_ref.at[at, 1:, side], sems.at[at, 2 + side]
                )
            )
        return found

    for at in range(size):
        for copy in copies(at):
            copy.start()
    for group in range(groups):
        for pair in range(seqs_heads):
            s, h = pair // heads, pair % heads
            cat_ref[s * frames : (s + 1) * frames, group * cols + h * HD : group * cols + (h + 1) * HD] = (
                mixed_refs[group][pair]
            )
    for at in range(size):
        for copy in copies(at):
            copy.wait()
        span = pl.ds(pl.multiple_of((me ^ at) * block, block), block)
        summed = dot(cat_ref[...], weight_ref[at].reshape(groups * cols, block))
        out_ref[:, span] = (hidden_ref[:, span].astype(F32) + summed).astype(BF16)


def temporal_output(place, hidden, mixed, own, pieces):
    rows, width = hidden.shape
    cols = own.shape[0]
    groups = len(mixed)
    size = len(pieces) // 2
    block = width // size

    def body(place_ref, hidden_ref, *refs):
        refs = list(refs)
        output_body(
            place_ref,
            hidden_ref,
            refs[:groups],
            refs[groups : groups + 1],
            refs[groups + 1 : groups + 1 + 2 * size],
            refs[groups + 1 + 2 * size :],
        )

    return pl.pallas_call(
        body,
        in_specs=[SM, VM] + [VM] * groups + [ANY] * (1 + 2 * size),
        out_specs=VM,
        out_shape=jax.ShapeDtypeStruct((rows, width), BF16),
        scratch_shapes=[
            pltpu.VMEM((rows, groups * cols), BF16),
            pltpu.VMEM((size, groups, 2, cols // 2, block), BF16),
            pltpu.SemaphoreType.DMA((size, 4)),
        ],
        compiler_params=PARAMS,
        cost_estimate=cost(2 * rows * groups * cols * width, 2 * groups * cols * width),
    )(place, hidden, *mixed, own, *pieces)


def put_qkv(normed, weights, part, out_ref, book, rows_out):
    books, block, wide = out_ref.shape
    cols = wide // 3
    for which in range(3):
        result = dot(normed, weights[which]).astype(BF16)
        for at in range(books):
            slot = lax.rem(at + books - book, books)
            out_ref[slot, :, which * cols : (which + 1) * cols] = result[at * block : (at + 1) * block]


def stream_kernel(place, temporal, pieces, entry, gain, weights, books, chunks):
    rows, width = temporal.shape
    size = len(pieces) // 2
    half, deep = pieces[0].shape
    block = rows // books
    cols = deep // chunks
    chips = size // 2

    def body(place_ref, temporal_ref, entry_ref, gain_ref, qkv_ref, *refs):
        piece_refs = refs[: 2 * size]
        stream_ref, normed_ref, out_ref, weight_ref, qkv_buf, acc_ref, sems, qkv_sem = refs[2 * size :]
        me = place_ref[0]
        book = place_ref[1]

        def copies(chip):
            found = []
            for core in range(2):
                at = 2 * chip + core
                where = (me ^ at) & 1
                for side in range(2):
                    found.append(
                        pltpu.make_async_copy(
                            piece_refs[2 * at + side],
                            weight_ref.at[chip, where, side],
                            sems.at[chip, 2 * core + side],
                        )
                    )
            return found

        fetch = pltpu.make_async_copy(qkv_ref.at[:, :, 0:cols], qkv_buf, qkv_sem.at[0])
        for chip in range(chips):
            for copy in copies(chip):
                copy.start()
        fetch.start()
        for chip in range(chips):
            for copy in copies(chip):
                copy.wait()
            start = pl.multiple_of(lax.shift_right_logical(me ^ (2 * chip), 1) * 4 * half, 4 * half)
            term = dot(temporal_ref[:, pl.ds(start, 4 * half)], weight_ref[chip].reshape(4 * half, deep))
            if chip == 0:
                acc_ref[...] = term
            else:
                acc_ref[...] += term
        stream = (acc_ref[...] + entry_ref[...].astype(F32)).astype(BF16)
        stream_ref[...] = stream
        values = stream.astype(F32)
        mean_sq = jnp.mean(values * values, axis=-1, keepdims=True)
        normed_ref[...] = (values * lax.rsqrt(mean_sq + EPS) * gain_ref[...]).astype(BF16)
        fetch.wait()
        put_qkv(normed_ref[...], qkv_buf, 0, out_ref, book, block)

    return pl.pallas_call(
        body,
        in_specs=[SM, VM, VM, VM, ANY] + [ANY] * (2 * size),
        out_specs=[VM, VM, VM],
        out_shape=[
            jax.ShapeDtypeStruct((rows, deep), BF16),
            jax.ShapeDtypeStruct((rows, deep), BF16),
            jax.ShapeDtypeStruct((books, block, 3 * cols), BF16),
        ],
        scratch_shapes=[
            pltpu.VMEM((chips, 2, 2, half, deep), BF16),
            pltpu.VMEM((3, deep, cols), BF16),
            pltpu.VMEM((rows, deep), F32),
            pltpu.SemaphoreType.DMA((chips, 4)),
            pltpu.SemaphoreType.DMA((1,)),
        ],
        compiler_params=PARAMS,
        cost_estimate=cost(2 * rows * width * deep + 6 * rows * deep * cols, 2 * width * deep + 6 * deep * cols),
    )(place, temporal, entry, gain, weights, *pieces)


def qkv_kernel(place, normed, weights, books, part, chunks):
    rows, deep = normed.shape
    cols = deep // chunks
    block = rows // books

    def body(place_ref, normed_ref, qkv_ref, out_ref):
        put_qkv(normed_ref[...], qkv_ref, part, out_ref, place_ref[1], block)

    return pl.pallas_call(
        body,
        grid=(1,),
        in_specs=[
            SM,
            pl.BlockSpec((rows, deep), lambda i: (0, 0)),
            pl.BlockSpec((3, deep, cols), lambda i: (0, 0, part)),
        ],
        out_specs=pl.BlockSpec((books, block, 3 * cols), lambda i: (0, 0, 0)),
        out_shape=jax.ShapeDtypeStruct((books, block, 3 * cols), BF16),
        compiler_params=PARAMS,
        cost_estimate=cost(6 * rows * deep * cols, 6 * deep * cols),
    )(place, normed, weights)


def two(values):
    high = values.astype(BF16)
    return high, (values - high.astype(F32)).astype(BF16)


def depth_attention(place, arrived):
    books = len(arrived)
    rows, wide = arrived[0].shape
    cols = wide // 3
    scale = 1.0 / (DHD**0.5)

    def body(place_ref, *refs):
        arrived_refs = refs[:books]
        out_ref, all_ref, result_ref = refs[books:]
        book = place_ref[1]
        for at in range(books):
            all_ref[lax.rem(book + books - at, books)] = arrived_refs[at][...]
        lane = lax.broadcasted_iota(jnp.int32, (cols, 128), 0) // DHD
        head = lax.broadcasted_iota(jnp.int32, (cols, 128), 1)
        gather = (lane == head).astype(BF16)
        lane_t = lax.broadcasted_iota(jnp.int32, (128, cols), 1) // DHD
        head_t = lax.broadcasted_iota(jnp.int32, (128, cols), 0)
        scatter = (lane_t == head_t).astype(BF16)
        for c in range(books):
            query = all_ref[c, :, :cols].astype(F32)
            scores = []
            for j in range(c + 1):
                high, low = two(query * all_ref[j, :, cols : 2 * cols].astype(F32))
                scores.append((dot(high, gather) + dot(low, gather)) * scale)
            highest = functools.reduce(jnp.maximum, scores)
            weights = [jnp.exp(score - highest) for score in scores]
            inverse = 1.0 / functools.reduce(jnp.add, weights)
            mixed = jnp.zeros((rows, cols), F32)
            for j in range(c + 1):
                mixed += dot(weights[j].astype(BF16), scatter) * all_ref[j, :, 2 * cols :].astype(F32)
            high, low = two(inverse)
            mixed = mixed * (dot(high, scatter) + dot(low, scatter))
            result_ref[c] = mixed.astype(BF16)
        for at in range(books):
            out_ref[at] = result_ref[lax.rem(book + at, books)]

    return pl.pallas_call(
        body,
        in_specs=[SM] + [VM] * books,
        out_specs=VM,
        out_shape=jax.ShapeDtypeStruct((books, rows, cols), BF16),
        scratch_shapes=[pltpu.VMEM((books, rows, wide), BF16), pltpu.VMEM((books, rows, cols), BF16)],
        compiler_params=PARAMS,
        cost_estimate=cost(4 * books * books * rows * cols * 128, 8 * books * rows * cols),
    )(place, *arrived)


def depth_output(place, stream, returned, weight):
    rows, deep = stream.shape
    chunks = len(returned)
    books = len(returned[0])
    block = rows // books
    cols = deep // chunks
    flat = [value for part in returned for value in part]

    def body(place_ref, stream_ref, weight_ref, *refs):
        parts = refs[: chunks * books]
        out_ref, cat_ref = refs[chunks * books :]
        book = place_ref[1]
        for k in range(chunks):
            for at in range(books):
                row = pl.multiple_of(lax.rem(book + books - at, books) * block, block)
                cat_ref[pl.ds(row, block), k * cols : (k + 1) * cols] = parts[k * books + at][...]
        result = dot(cat_ref[...], weight_ref[...]) + stream_ref[...].astype(F32)
        out_ref[...] = result.astype(BF16)

    return pl.pallas_call(
        body,
        in_specs=[SM] + [VM] * (2 + chunks * books),
        out_specs=VM,
        out_shape=jax.ShapeDtypeStruct((rows, deep), BF16),
        scratch_shapes=[pltpu.VMEM((rows, deep), BF16)],
        compiler_params=PARAMS,
        cost_estimate=cost(2 * rows * deep * deep, 2 * deep * deep),
    )(place, stream, weight, *flat)


def shards(
    hidden,
    temporal_gain,
    temporal_qkv,
    temporal_out,
    codebook_ids,
    embedding,
    input_weight,
    depth_gain,
    depth_qkv,
    depth_out,
):
    seqs, frames, width = hidden.shape
    rows = seqs * frames
    deep = depth_gain.shape[1]
    cols = temporal_out.shape[0]
    size = lax.axis_size("seq")
    books = lax.axis_size("cb")
    place = jnp.stack([lax.axis_index("seq"), lax.axis_index("cb")]).astype(jnp.int32)

    block = width // size
    ring = [lax.dynamic_slice_in_dim(temporal_out, lax.axis_index("seq") * block, block, 1)]
    for _ in range(books - 1):
        ring.append(shift(ring[-1], "cb", 1))
    in_rows = input_weight.shape[1]
    in_pieces = spread_halves(
        input_weight[0, : in_rows // 2], input_weight[0, in_rows // 2 :], "seq"
    )
    foreign = jnp.stack(ring[1:])
    out_pieces = spread_halves(foreign[:, : cols // 2], foreign[:, cols // 2 :], "seq")

    entry = jnp.take(embedding[0], codebook_ids.reshape(rows), axis=0)

    packed = project(hidden, temporal_gain, temporal_qkv)
    own_mixed = temporal_attention(packed)
    mixed = [own_mixed] + [shift(own_mixed, "cb", by) for by in range(1, books)]
    temporal = temporal_output(place, hidden.reshape(rows, width), mixed, temporal_out, out_pieces)

    stream, normed, first = stream_kernel(
        place, temporal, in_pieces, entry, depth_gain, depth_qkv[0], books, CHUNKS
    )
    returned = []
    for part in range(CHUNKS):
        sent = first if part == 0 else qkv_kernel(place, normed, depth_qkv[0], books, part, CHUNKS)
        arrived = [sent[0]] + [shift(sent[by], "cb", by) for by in range(1, books)]
        result = depth_attention(place, arrived)
        returned.append([result[0]] + [shift(result[by], "cb", by) for by in range(1, books)])
    depth = depth_output(place, stream, returned, depth_out[0])
    return (temporal.reshape(seqs, frames, width), depth.reshape(seqs, frames, 1, deep))


def solution(mesh):
    placed = (
        P(None, "seq", None),
        P(),
        P(None, None, "cb"),
        P("cb", None),
        P(None, "seq", "cb"),
        P("cb", None, None),
        P("cb", "seq", None),
        P("cb", None),
        P("cb", None, None, None),
        P("cb", None, None),
    )
    return jax.shard_map(
        shards,
        mesh=mesh,
        in_specs=placed,
        out_specs=(P(None, "seq", None), P(None, "seq", "cb", None)),
        check_vma=False,
    )
```

```python
import functools

import jax
import jax.numpy as jnp
from jax import lax
from jax.experimental import pallas as pl
from jax.experimental.pallas import tpu as pltpu
from jax.sharding import PartitionSpec as P


HD = 128
DHD = 64
EPS = 1e-05
NEG = -1e30
F32 = jnp.float32
BF16 = jnp.bfloat16
CHUNKS = 2
VMEM_LIMIT = 60 * 1024 * 1024


VM = pl.BlockSpec(memory_space=pltpu.VMEM)
SM = pl.BlockSpec(memory_space=pltpu.SMEM)
ANY = pl.BlockSpec(memory_space=pl.ANY)
PARAMS = pltpu.CompilerParams(vmem_limit_bytes=VMEM_LIMIT)


def cost(flops, moved):
    return pl.CostEstimate(flops=flops, bytes_accessed=moved, transcendentals=0)


def dot(a, b):
    return jnp.dot(a, b, preferred_element_type=F32)


def flip(x, axis, bit):
    return lax.ppermute(x, axis, [(i, i ^ bit) for i in range(lax.axis_size(axis))])


def shift(x, axis, by):
    size = lax.axis_size(axis)
    return lax.ppermute(x, axis, [(i, (i + by) % size) for i in range(size)])


def ici_bits(size):
    return [1 << place for place in range(1, size.bit_length() - 1)]


def spread(piece, axis, order):
    held = {0: piece}
    for bit in order:
        held.update({at ^ bit: flip(v, axis, bit) for at, v in list(held.items())})
    held.update({at ^ 1: flip(v, axis, 1) for at, v in list(held.items())})
    return held


def spread_halves(first, second, axis):
    size = lax.axis_size(axis)
    a = spread(first, axis, ici_bits(size))
    b = spread(second, axis, ici_bits(size)[::-1])
    return [half for at in range(size) for half in (a[at], b[at])]


def project_body(hidden_ref, gain_ref, weight_ref, out_ref, normed_ref):
    seqs, heads, frames, _ = out_ref.shape
    rows = normed_ref.shape[0]
    step = min(64, rows)

    @pl.when(pl.program_id(0) == 0)
    def _():
        def one(at, carry):
            span = pl.ds(pl.multiple_of(at * step, step), step)
            values = hidden_ref[span, :].astype(F32)
            mean_sq = jnp.mean(values * values, axis=-1, keepdims=True)
            normed_ref[span, :] = (values * lax.rsqrt(mean_sq + EPS) * gain_ref[...]).astype(BF16)
            return carry

        lax.fori_loop(0, rows // step, one, 0)

    result = dot(normed_ref[...], weight_ref[0]).astype(BF16)
    for s in range(seqs):
        for h in range(heads):
            out_ref[s, h] = result[s * frames : (s + 1) * frames, h * HD : (h + 1) * HD]


def project(hidden, gain, weight):
    seqs, frames, width = hidden.shape
    cols = weight.shape[2]
    heads = cols // HD
    per = min(2, heads)
    parts = heads // per
    rows = seqs * frames
    return pl.pallas_call(
        project_body,
        grid=(3 * parts,),
        in_specs=[
            pl.BlockSpec((rows, width), lambda i: (0, 0)),
            pl.BlockSpec((1, width), lambda i: (0, 0)),
            pl.BlockSpec((1, width, per * HD), lambda i: (i // parts, 0, i % parts)),
        ],
        out_specs=pl.BlockSpec((seqs, per, frames, HD), lambda i: (0, i % parts, 0, i // parts)),
        out_shape=jax.ShapeDtypeStruct((seqs, heads, frames, 3 * HD), BF16),
        scratch_shapes=[pltpu.VMEM((rows, width), BF16)],
        compiler_params=PARAMS,
        cost_estimate=cost(6 * rows * width * cols, 6 * width * cols + 2 * rows * width),
    )(hidden.reshape(rows, width), gain.reshape(1, width), weight)


def attend_body(packed_ref, out_ref):
    length = packed_ref.shape[0]
    block = min(256, length)
    scale = 1.0 / (HD**0.5)
    for start in range(0, length, block):
        stop = start + block
        scores = (
            lax.dot_general(
                packed_ref[start:stop, :HD],
                packed_ref[:stop, HD : 2 * HD],
                (((1,), (1,)), ((), ())),
                preferred_element_type=F32,
            )
            * scale
        )
        rows = lax.broadcasted_iota(jnp.int32, scores.shape, 0) + start
        cols = lax.broadcasted_iota(jnp.int32, scores.shape, 1)
        scores = jnp.where(cols <= rows, scores, NEG)
        weights = jnp.exp(scores - jnp.max(scores, axis=-1, keepdims=True))
        totals = jnp.sum(weights, axis=-1, keepdims=True)
        mixed = dot(weights.astype(BF16), packed_ref[:stop, 2 * HD :])
        out_ref[start:stop, :] = (mixed / totals).astype(BF16)


def attend_pair(packed):
    length = packed.shape[0]
    return pl.pallas_call(
        attend_body,
        in_specs=[VM],
        out_specs=VM,
        out_shape=jax.ShapeDtypeStruct((length, HD), BF16),
        compiler_params=PARAMS,
        cost_estimate=cost(3 * length * length * HD, 8 * length * HD),
    )(packed)


def temporal_attention(packed):
    seqs, heads, frames, _ = packed.shape
    pairs = seqs * heads
    size = lax.axis_size("seq")
    if pairs == size:
        whole = lax.all_to_all(packed.reshape(pairs, frames, 3 * HD), "seq", split_axis=0, concat_axis=0, tiled=True)
        mixed = attend_pair(whole.reshape(size * frames, 3 * HD))
        return lax.all_to_all(
            mixed.reshape(size, frames, HD), "seq", split_axis=0, concat_axis=0, tiled=True
        )
    queries = packed[..., :HD]
    both = lax.all_gather(packed[..., HD:], "seq", axis=2, tiled=True)
    keys, values = both[..., :HD], both[..., HD:]
    scores = jnp.einsum("shqd,shkd->shqk", queries, keys, preferred_element_type=F32) / (HD**0.5)
    at = lax.axis_index("seq") * frames + jnp.arange(frames, dtype=jnp.int32)
    allowed = jnp.arange(size * frames, dtype=jnp.int32)[None, :] <= at[:, None]
    scores = jnp.where(allowed, scores, NEG)
    weights = jnp.exp(scores - jnp.max(scores, axis=-1, keepdims=True))
    totals = jnp.sum(weights, axis=-1, keepdims=True)
    mixed = jnp.einsum(
        "shqk,shkd->shqd", weights.astype(BF16), values, preferred_element_type=F32
    )
    return (mixed / totals).astype(BF16).reshape(pairs, frames, HD)


def output_body(place_ref, hidden_ref, *refs):
    books = place_ref.shape[0] - 2
    del books
    mixed_refs, (own_ref,), pieces, (out_ref, cat_ref, weight_ref, sems) = refs
    size, groups, _, half, block = weight_ref.shape
    seqs_heads, frames, _ = mixed_refs[0].shape
    cols = 2 * half
    heads = cols // HD
    me = place_ref[0]

    def copies(at):
        column = pl.multiple_of((me ^ at) * block, block)
        found = []
        for side in range(2):
            found.append(
                pltpu.make_async_copy(
                    own_ref.at[side * half : (side + 1) * half, pl.ds(column, block)],
                    weight_ref.at[at, 0, side],
                    sems.at[at, side],
                )
            )
            found.append(
                pltpu.make_async_copy(
                    pieces[2 * at + side], weight_ref.at[at, 1:, side], sems.at[at, 2 + side]
                )
            )
        return found

    for at in range(size):
        for copy in copies(at):
            copy.start()
    for group in range(groups):
        for pair in range(seqs_heads):
            s, h = pair // heads, pair % heads
            cat_ref[s * frames : (s + 1) * frames, group * cols + h * HD : group * cols + (h + 1) * HD] = (
                mixed_refs[group][pair]
            )
    for at in range(size):
        for copy in copies(at):
            copy.wait()
        span = pl.ds(pl.multiple_of((me ^ at) * block, block), block)
        summed = dot(cat_ref[...], weight_ref[at].reshape(groups * cols, block))
        out_ref[:, span] = (hidden_ref[:, span].astype(F32) + summed).astype(BF16)


def temporal_output(place, hidden, mixed, own, pieces):
    rows, width = hidden.shape
    cols = own.shape[0]
    groups = len(mixed)
    size = len(pieces) // 2
    block = width // size

    def body(place_ref, hidden_ref, *refs):
        refs = list(refs)
        output_body(
            place_ref,
            hidden_ref,
            refs[:groups],
            refs[groups : groups + 1],
            refs[groups + 1 : groups + 1 + 2 * size],
            refs[groups + 1 + 2 * size :],
        )

    return pl.pallas_call(
        body,
        in_specs=[SM, VM] + [VM] * groups + [ANY] * (1 + 2 * size),
        out_specs=VM,
        out_shape=jax.ShapeDtypeStruct((rows, width), BF16),
        scratch_shapes=[
            pltpu.VMEM((rows, groups * cols), BF16),
            pltpu.VMEM((size, groups, 2, cols // 2, block), BF16),
            pltpu.SemaphoreType.DMA((size, 4)),
        ],
        compiler_params=PARAMS,
        cost_estimate=cost(2 * rows * groups * cols * width, 2 * groups * cols * width),
    )(place, hidden, *mixed, own, *pieces)


def put_qkv(normed, weights, out_refs, full_ref, book):
    books = len(out_refs)
    block, wide = out_refs[0].shape
    cols = wide // 3
    for which in range(3):
        full_ref[:, which * cols : (which + 1) * cols] = dot(normed, weights[which])
    for at in range(books):
        row = pl.multiple_of(lax.rem(book + at, books) * block, block)
        out_refs[at][...] = full_ref[pl.ds(row, block), :].astype(BF16)


def stream_kernel(place, temporal, pieces, entry, gain, weights, books, chunks):
    rows, width = temporal.shape
    size = len(pieces) // 2
    half, deep = pieces[0].shape
    block = rows // books
    cols = deep // chunks
    chips = size // 2

    def body(place_ref, temporal_ref, entry_ref, gain_ref, qkv_ref, *refs):
        piece_refs = refs[: 2 * size]
        stream_ref, normed_ref = refs[2 * size : 2 * size + 2]
        out_refs = refs[2 * size + 2 : 2 * size + 2 + books]
        weight_ref, qkv_buf, acc_ref, full_ref, sems, qkv_sem = refs[2 * size + 2 + books :]
        me = place_ref[0]
        book = place_ref[1]

        def copies(chip):
            found = []
            for core in range(2):
                at = 2 * chip + core
                where = (me ^ at) & 1
                for side in range(2):
                    found.append(
                        pltpu.make_async_copy(
                            piece_refs[2 * at + side],
                            weight_ref.at[chip, where, side],
                            sems.at[chip, 2 * core + side],
                        )
                    )
            return found

        fetch = pltpu.make_async_copy(qkv_ref.at[:, :, 0:cols], qkv_buf, qkv_sem.at[0])
        for chip in range(chips):
            for copy in copies(chip):
                copy.start()
        fetch.start()
        for chip in range(chips):
            for copy in copies(chip):
                copy.wait()
            start = pl.multiple_of(lax.shift_right_logical(me ^ (2 * chip), 1) * 4 * half, 4 * half)
            term = dot(temporal_ref[:, pl.ds(start, 4 * half)], weight_ref[chip].reshape(4 * half, deep))
            if chip == 0:
                acc_ref[...] = term
            else:
                acc_ref[...] += term
        stream = (acc_ref[...] + entry_ref[...].astype(F32)).astype(BF16)
        stream_ref[...] = stream
        values = stream.astype(F32)
        mean_sq = jnp.mean(values * values, axis=-1, keepdims=True)
        normed_ref[...] = (values * lax.rsqrt(mean_sq + EPS) * gain_ref[...]).astype(BF16)
        fetch.wait()
        put_qkv(normed_ref[...], qkv_buf, out_refs, full_ref, book)

    return pl.pallas_call(
        body,
        in_specs=[SM, VM, VM, VM, ANY] + [ANY] * (2 * size),
        out_specs=[VM] * (2 + books),
        out_shape=[jax.ShapeDtypeStruct((rows, deep), BF16)] * 2
        + [jax.ShapeDtypeStruct((block, 3 * cols), BF16)] * books,
        scratch_shapes=[
            pltpu.VMEM((chips, 2, 2, half, deep), BF16),
            pltpu.VMEM((3, deep, cols), BF16),
            pltpu.VMEM((rows, deep), F32),
            pltpu.VMEM((rows, 3 * cols), F32),
            pltpu.SemaphoreType.DMA((chips, 4)),
            pltpu.SemaphoreType.DMA((1,)),
        ],
        compiler_params=PARAMS,
        cost_estimate=cost(2 * rows * width * deep + 6 * rows * deep * cols, 2 * width * deep + 6 * deep * cols),
    )(place, temporal, entry, gain, weights, *pieces)


def qkv_kernel(place, normed, weights, books, part, chunks):
    rows, deep = normed.shape
    cols = deep // chunks
    block = rows // books

    def body(place_ref, normed_ref, qkv_ref, *refs):
        put_qkv(normed_ref[...], qkv_ref, refs[:books], refs[books], place_ref[1])

    return pl.pallas_call(
        body,
        grid=(1,),
        in_specs=[
            SM,
            pl.BlockSpec((rows, deep), lambda i: (0, 0)),
            pl.BlockSpec((3, deep, cols), lambda i: (0, 0, part)),
        ],
        out_specs=[pl.BlockSpec((block, 3 * cols), lambda i: (0, 0))] * books,
        out_shape=[jax.ShapeDtypeStruct((block, 3 * cols), BF16)] * books,
        scratch_shapes=[pltpu.VMEM((rows, 3 * cols), F32)],
        compiler_params=PARAMS,
        cost_estimate=cost(6 * rows * deep * cols, 6 * deep * cols),
    )(place, normed, weights)


def two(values):
    high = values.astype(BF16)
    return high, (values - high.astype(F32)).astype(BF16)


def depth_attention(place, arrived):
    books = len(arrived)
    rows, wide = arrived[0].shape
    cols = wide // 3
    scale = 1.0 / (DHD**0.5)

    def body(place_ref, *refs):
        arrived_refs = refs[:books]
        out_refs = refs[books : 2 * books]
        all_ref, result_ref = refs[2 * books :]
        book = place_ref[1]
        for at in range(books):
            all_ref[lax.rem(book + books - at, books)] = arrived_refs[at][...]
        lane = lax.broadcasted_iota(jnp.int32, (cols, 128), 0) // DHD
        head = lax.broadcasted_iota(jnp.int32, (cols, 128), 1)
        gather = (lane == head).astype(BF16)
        lane_t = lax.broadcasted_iota(jnp.int32, (128, cols), 1) // DHD
        head_t = lax.broadcasted_iota(jnp.int32, (128, cols), 0)
        scatter = (lane_t == head_t).astype(BF16)
        for c in range(books):
            query = all_ref[c, :, :cols].astype(F32)
            scores = []
            for j in range(c + 1):
                high, low = two(query * all_ref[j, :, cols : 2 * cols].astype(F32))
                scores.append((dot(high, gather) + dot(low, gather)) * scale)
            highest = functools.reduce(jnp.maximum, scores)
            weights = [jnp.exp(score - highest) for score in scores]
            inverse = 1.0 / functools.reduce(jnp.add, weights)
            mixed = jnp.zeros((rows, cols), F32)
            for j in range(c + 1):
                mixed += dot(weights[j].astype(BF16), scatter) * all_ref[j, :, 2 * cols :].astype(F32)
            high, low = two(inverse)
            mixed = mixed * (dot(high, scatter) + dot(low, scatter))
            result_ref[c] = mixed.astype(BF16)
        for at in range(books):
            out_refs[at][...] = result_ref[lax.rem(book + at, books)]

    return pl.pallas_call(
        body,
        in_specs=[SM] + [VM] * books,
        out_specs=[VM] * books,
        out_shape=[jax.ShapeDtypeStruct((rows, cols), BF16)] * books,
        scratch_shapes=[pltpu.VMEM((books, rows, wide), BF16), pltpu.VMEM((books, rows, cols), BF16)],
        compiler_params=PARAMS,
        cost_estimate=cost(4 * books * books * rows * cols * 128, 8 * books * rows * cols),
    )(place, *arrived)


def depth_output(place, stream, returned, weight):
    rows, deep = stream.shape
    chunks = len(returned)
    books = len(returned[0])
    block = rows // books
    cols = deep // chunks
    flat = [value for part in returned for value in part]

    def body(place_ref, stream_ref, weight_ref, *refs):
        parts = refs[: chunks * books]
        out_ref, cat_ref = refs[chunks * books :]
        book = place_ref[1]
        for k in range(chunks):
            for at in range(books):
                row = pl.multiple_of(lax.rem(book + books - at, books) * block, block)
                cat_ref[pl.ds(row, block), k * cols : (k + 1) * cols] = parts[k * books + at][...]
        result = dot(cat_ref[...], weight_ref[...]) + stream_ref[...].astype(F32)
        out_ref[...] = result.astype(BF16)

    return pl.pallas_call(
        body,
        in_specs=[SM] + [VM] * (2 + chunks * books),
        out_specs=VM,
        out_shape=jax.ShapeDtypeStruct((rows, deep), BF16),
        scratch_shapes=[pltpu.VMEM((rows, deep), BF16)],
        compiler_params=PARAMS,
        cost_estimate=cost(2 * rows * deep * deep, 2 * deep * deep),
    )(place, stream, weight, *flat)


def shards(
    hidden,
    temporal_gain,
    temporal_qkv,
    temporal_out,
    codebook_ids,
    embedding,
    input_weight,
    depth_gain,
    depth_qkv,
    depth_out,
):
    seqs, frames, width = hidden.shape
    rows = seqs * frames
    deep = depth_gain.shape[1]
    cols = temporal_out.shape[0]
    size = lax.axis_size("seq")
    books = lax.axis_size("cb")
    place = jnp.stack([lax.axis_index("seq"), lax.axis_index("cb")]).astype(jnp.int32)

    block = width // size
    ring = [lax.dynamic_slice_in_dim(temporal_out, lax.axis_index("seq") * block, block, 1)]
    for _ in range(1, books):
        ring.append(shift(ring[-1], "cb", 1))
    half = input_weight.shape[1] // 2
    in_pieces = spread_halves(input_weight[0, :half], input_weight[0, half:], "seq")
    half = cols // 2
    first = jnp.stack([piece[:half] for piece in ring[1:]])
    second = jnp.stack([piece[half:] for piece in ring[1:]])
    out_pieces = spread_halves(first, second, "seq")

    entry = jnp.take(embedding[0], codebook_ids.reshape(rows), axis=0)

    packed = project(hidden, temporal_gain, temporal_qkv)
    own_mixed = temporal_attention(packed)
    mixed = [own_mixed] + [shift(own_mixed, "cb", by) for by in range(1, books)]
    temporal = temporal_output(
        place, hidden.reshape(rows, width), mixed, temporal_out, out_pieces
    )
    stream, normed, *sent = stream_kernel(place, temporal, in_pieces, entry, depth_gain, depth_qkv[0], books, CHUNKS)
    arrived, returned = [], []
    for part in range(CHUNKS):
        if part > 0:
            sent = qkv_kernel(place, normed, depth_qkv[0], books, part, CHUNKS)
        arrived.append([sent[0]] + [shift(sent[by], "cb", by) for by in range(1, books)])
    for part in range(CHUNKS):
        result = depth_attention(place, arrived[part])
        returned.append([result[0]] + [shift(result[by], "cb", by) for by in range(1, books)])
    depth = depth_output(place, stream, returned, depth_out[0])
    return (temporal.reshape(seqs, frames, width), depth.reshape(seqs, frames, 1, deep))


def solution(mesh):
    placed = (
        P(None, "seq", None),
        P(),
        P(None, None, "cb"),
        P("cb", None),
        P(None, "seq", "cb"),
        P("cb", None, None),
        P("cb", "seq", None),
        P("cb", None),
        P("cb", None, None, None),
        P("cb", None, None),
    )
    return jax.shard_map(
        shards,
        mesh=mesh,
        in_specs=placed,
        out_specs=(P(None, "seq", None), P(None, "seq", "cb", None)),
        check_vma=False,
    )
```

```python
import functools

import jax
import jax.numpy as jnp
from jax import lax
from jax.experimental import pallas as pl
from jax.experimental.pallas import tpu as pltpu
from jax.sharding import PartitionSpec as P


HD = 128
DHD = 64
EPS = 1e-05
NEG = -1e30
F32 = jnp.float32
BF16 = jnp.bfloat16
CHUNKS = 2
VMEM_LIMIT = 32 * 1024 * 1024
EARLY_LIMIT = 40 * 1024 * 1024
LATE_LIMIT = 32 * 1024 * 1024


VM = pl.BlockSpec(memory_space=pltpu.VMEM)
SM = pl.BlockSpec(memory_space=pltpu.SMEM)
ANY = pl.BlockSpec(memory_space=pl.ANY)
PARAMS = pltpu.CompilerParams(vmem_limit_bytes=VMEM_LIMIT)


def cost(flops, moved):
    return pl.CostEstimate(flops=flops, bytes_accessed=moved, transcendentals=0)


def dot(a, b):
    return jnp.dot(a, b, preferred_element_type=F32)


def flip(x, axis, bit):
    return lax.ppermute(x, axis, [(i, i ^ bit) for i in range(lax.axis_size(axis))])


def shift(x, axis, by):
    size = lax.axis_size(axis)
    return lax.ppermute(x, axis, [(i, (i + by) % size) for i in range(size)])


def ici_bits(size):
    return [1 << place for place in range(1, size.bit_length() - 1)]


def spread(piece, axis, order):
    held = {0: piece}
    for bit in order:
        held.update({at ^ bit: flip(v, axis, bit) for at, v in list(held.items())})
    held.update({at ^ 1: flip(v, axis, 1) for at, v in list(held.items())})
    return held


def spread_halves(first, second, axis):
    size = lax.axis_size(axis)
    a = spread(first, axis, ici_bits(size))
    b = spread(second, axis, ici_bits(size)[::-1])
    return [half for at in range(size) for half in (a[at], b[at])]


def project_body(hidden_ref, gain_ref, weight_ref, out_ref, normed_ref):
    seqs, heads, frames, _ = out_ref.shape
    rows = normed_ref.shape[0]
    step = min(64, rows)

    @pl.when(pl.program_id(0) == 0)
    def _():
        def one(at, carry):
            span = pl.ds(pl.multiple_of(at * step, step), step)
            values = hidden_ref[span, :].astype(F32)
            mean_sq = jnp.mean(values * values, axis=-1, keepdims=True)
            normed_ref[span, :] = (values * lax.rsqrt(mean_sq + EPS) * gain_ref[...]).astype(BF16)
            return carry

        lax.fori_loop(0, rows // step, one, 0)

    result = dot(normed_ref[...], weight_ref[0]).astype(BF16)
    for s in range(seqs):
        for h in range(heads):
            out_ref[s, h] = result[s * frames : (s + 1) * frames, h * HD : (h + 1) * HD]


def project(hidden, gain, weight):
    seqs, frames, width = hidden.shape
    cols = weight.shape[2]
    heads = cols // HD
    per = min(2, heads)
    parts = heads // per
    rows = seqs * frames
    return pl.pallas_call(
        project_body,
        grid=(3 * parts,),
        in_specs=[
            pl.BlockSpec((rows, width), lambda i: (0, 0)),
            pl.BlockSpec((1, width), lambda i: (0, 0)),
            pl.BlockSpec((1, width, per * HD), lambda i: (i // parts, 0, i % parts)),
        ],
        out_specs=pl.BlockSpec((seqs, per, frames, HD), lambda i: (0, i % parts, 0, i // parts)),
        out_shape=jax.ShapeDtypeStruct((seqs, heads, frames, 3 * HD), BF16),
        scratch_shapes=[pltpu.VMEM((rows, width), BF16)],
        compiler_params=PARAMS,
        cost_estimate=cost(6 * rows * width * cols, 6 * width * cols + 2 * rows * width),
    )(hidden.reshape(rows, width), gain.reshape(1, width), weight)


def attend_body(packed_ref, out_ref):
    length = packed_ref.shape[0]
    block = min(256, length)
    scale = 1.0 / (HD**0.5)
    for start in range(0, length, block):
        stop = start + block
        scores = (
            lax.dot_general(
                packed_ref[start:stop, :HD],
                packed_ref[:stop, HD : 2 * HD],
                (((1,), (1,)), ((), ())),
                preferred_element_type=F32,
            )
            * scale
        )
        rows = lax.broadcasted_iota(jnp.int32, scores.shape, 0) + start
        cols = lax.broadcasted_iota(jnp.int32, scores.shape, 1)
        scores = jnp.where(cols <= rows, scores, NEG)
        weights = jnp.exp(scores - jnp.max(scores, axis=-1, keepdims=True))
        totals = jnp.sum(weights, axis=-1, keepdims=True)
        mixed = dot(weights.astype(BF16), packed_ref[:stop, 2 * HD :])
        out_ref[start:stop, :] = (mixed / totals).astype(BF16)


def attend_pair(packed):
    length = packed.shape[0]
    return pl.pallas_call(
        attend_body,
        in_specs=[VM],
        out_specs=VM,
        out_shape=jax.ShapeDtypeStruct((length, HD), BF16),
        compiler_params=PARAMS,
        cost_estimate=cost(3 * length * length * HD, 8 * length * HD),
    )(packed)


def temporal_attention(packed):
    seqs, heads, frames, _ = packed.shape
    pairs = seqs * heads
    size = lax.axis_size("seq")
    if pairs == size:
        whole = lax.all_to_all(packed.reshape(pairs, frames, 3 * HD), "seq", split_axis=0, concat_axis=0, tiled=True)
        mixed = attend_pair(whole.reshape(size * frames, 3 * HD))
        return lax.all_to_all(
            mixed.reshape(size, frames, HD), "seq", split_axis=0, concat_axis=0, tiled=True
        )
    queries = packed[..., :HD]
    both = lax.all_gather(packed[..., HD:], "seq", axis=2, tiled=True)
    keys, values = both[..., :HD], both[..., HD:]
    scores = jnp.einsum("shqd,shkd->shqk", queries, keys, preferred_element_type=F32) / (HD**0.5)
    at = lax.axis_index("seq") * frames + jnp.arange(frames, dtype=jnp.int32)
    allowed = jnp.arange(size * frames, dtype=jnp.int32)[None, :] <= at[:, None]
    scores = jnp.where(allowed, scores, NEG)
    weights = jnp.exp(scores - jnp.max(scores, axis=-1, keepdims=True))
    totals = jnp.sum(weights, axis=-1, keepdims=True)
    mixed = jnp.einsum(
        "shqk,shkd->shqd", weights.astype(BF16), values, preferred_element_type=F32
    )
    return (mixed / totals).astype(BF16).reshape(pairs, frames, HD)


def put_mixed(mixed_refs, cat_ref):
    pairs, frames, _ = mixed_refs[0].shape
    cols = cat_ref.shape[1] // len(mixed_refs)
    heads = cols // HD
    for group, ref in enumerate(mixed_refs):
        for pair in range(pairs):
            s, h = pair // heads, pair % heads
            at = group * cols + h * HD
            cat_ref[s * frames : (s + 1) * frames, at : at + HD] = ref[pair]


def chip_start(me, at, wide):
    return pl.multiple_of(lax.shift_right_logical(me ^ at, 1) * wide, wide)


def early_output(place, hidden, mixed, own, out_pieces, in_pieces, late):
    rows, width = hidden.shape
    cols = own.shape[0]
    groups = len(mixed)
    size = len(out_pieces) // 2
    block = width // size
    half, deep = in_pieces[0].shape
    chips = [at for at in range(0, size, 2) if at != late]
    count = len(chips)
    used = [2 * (at + core) + side for at in chips for core in range(2) for side in range(2)]

    def body(place_ref, hidden_ref, *refs):
        mixed_refs = refs[:groups]
        own_ref = refs[groups]
        outs = refs[groups + 1 : groups + 1 + 4 * count]
        ins = refs[groups + 1 + 4 * count : groups + 1 + 8 * count]
        out_ref, acc_ref, cat_ref, out_buf, in_buf, out_sems, in_sems = refs[groups + 1 + 8 * count :]
        me = place_ref[0]

        def out_copies(index):
            at = chips[index // 2] + index % 2
            column = pl.multiple_of((me ^ at) * block, block)
            found = []
            for side in range(2):
                found.append(
                    pltpu.make_async_copy(
                        own_ref.at[side * (cols // 2) : (side + 1) * (cols // 2), pl.ds(column, block)],
                        out_buf.at[index, 0, side],
                        out_sems.at[index, side],
                    )
                )
                found.append(
                    pltpu.make_async_copy(
                        outs[2 * index + side], out_buf.at[index, 1:, side], out_sems.at[index, 2 + side]
                    )
                )
            return found

        def in_copies(chip):
            found = []
            for core in range(2):
                where = (me ^ core) & 1
                for side in range(2):
                    found.append(
                        pltpu.make_async_copy(
                            ins[4 * chip + 2 * core + side],
                            in_buf.at[chip, where, side],
                            in_sems.at[chip, 2 * core + side],
                        )
                    )
            return found

        for index in range(2 * count):
            for copy in out_copies(index):
                copy.start()
        for chip in range(count):
            for copy in in_copies(chip):
                copy.start()
        put_mixed(mixed_refs, cat_ref)
        for index in range(2 * count):
            at = chips[index // 2] + index % 2
            for copy in out_copies(index):
                copy.wait()
            span = pl.ds(pl.multiple_of((me ^ at) * block, block), block)
            summed = dot(cat_ref[...], out_buf[index].reshape(groups * cols, block))
            out_ref[:, span] = (hidden_ref[:, span].astype(F32) + summed).astype(BF16)
        for chip in range(count):
            for copy in in_copies(chip):
                copy.wait()
            span = pl.ds(chip_start(me, chips[chip], 4 * half), 4 * half)
            term = dot(out_ref[:, span], in_buf[chip].reshape(4 * half, deep))
            if chip == 0:
                acc_ref[...] = term
            else:
                acc_ref[...] += term

    return pl.pallas_call(
        body,
        in_specs=[SM, VM] + [VM] * groups + [ANY] * (1 + 8 * count),
        out_specs=[VM, VM],
        out_shape=[
            jax.ShapeDtypeStruct((rows, width), BF16),
            jax.ShapeDtypeStruct((rows, deep), F32),
        ],
        scratch_shapes=[
            pltpu.VMEM((rows, groups * cols), BF16),
            pltpu.VMEM((2 * count, groups, 2, cols // 2, block), BF16),
            pltpu.VMEM((count, 2, 2, half, deep), BF16),
            pltpu.SemaphoreType.DMA((2 * count, 4)),
            pltpu.SemaphoreType.DMA((count, 4)),
        ],
        compiler_params=pltpu.CompilerParams(vmem_limit_bytes=EARLY_LIMIT),
        cost_estimate=cost(
            2 * rows * width * (groups * cols + deep), 2 * width * (groups * cols + deep)
        ),
    )(
        place,
        hidden,
        *mixed,
        own,
        *[out_pieces[i] for i in used],
        *[in_pieces[i] for i in used],
    )


def put_qkv(normed, weights, out_refs, full_ref, book):
    books = len(out_refs)
    block, wide = out_refs[0].shape
    cols = wide // 3
    for which in range(3):
        full_ref[:, which * cols : (which + 1) * cols] = dot(normed, weights[which])
    for at in range(books):
        row = pl.multiple_of(lax.rem(book + at, books) * block, block)
        out_refs[at][...] = full_ref[pl.ds(row, block), :].astype(BF16)


def late_output(place, early, acc, hidden, mixed, own, out_pieces, in_pieces, entry, gain, weights, late, chunks):
    rows, width = hidden.shape
    books = len(mixed)
    size = len(out_pieces) // 2
    cols = own.shape[0]
    block = width // size
    half, deep = in_pieces[0].shape
    part = deep // chunks
    share = rows // books
    used = [2 * (late + core) + side for core in range(2) for side in range(2)]

    def body(place_ref, _, acc_ref, hidden_ref, entry_ref, gain_ref, own_ref, qkv_ref, *refs):
        mixed_refs = refs[:books]
        outs = refs[books : books + 4]
        ins = refs[books + 4 : books + 8]
        out_ref, stream_ref, normed_ref = refs[books + 8 : books + 11]
        out_refs = refs[books + 11 : 2 * books + 11]
        cat_ref, own_buf, qkv_buf, full_ref, late_buf, sems = refs[2 * books + 11 :]
        me = place_ref[0]
        book = place_ref[1]
        start = chip_start(me, late, 2 * block)
        fetch_own = pltpu.make_async_copy(own_ref.at[:, pl.ds(start, 2 * block)], own_buf, sems.at[0])
        fetch_qkv = pltpu.make_async_copy(qkv_ref.at[:, :, 0:part], qkv_buf, sems.at[1])
        fetch_own.start()
        fetch_qkv.start()
        put_mixed(mixed_refs, cat_ref)
        fetch_own.wait()
        total = acc_ref[...] + entry_ref[...].astype(F32)
        for core in range(2):
            column = pl.multiple_of((me ^ (late + core)) * block, block)
            span = pl.ds(column, block)
            local = pl.ds(pl.multiple_of(((me ^ core) & 1) * block, block), block)
            summed = dot(cat_ref[:, :cols], own_buf[:, local])
            for side in range(2):
                for group in range(1, books):
                    at = group * cols + side * (cols // 2)
                    summed += dot(cat_ref[:, at : at + cols // 2], outs[2 * core + side][group - 1])
            value = (hidden_ref[:, span].astype(F32) + summed).astype(BF16)
            late_buf[:, local] = value
            for side in range(2):
                total += dot(value[:, side * half : (side + 1) * half], ins[2 * core + side][...])
        put = pltpu.make_async_copy(late_buf, out_ref.at[:, pl.ds(start, 2 * block)], sems.at[2])
        put.start()
        stream = total.astype(BF16)
        stream_ref[...] = stream
        values = stream.astype(F32)
        mean_sq = jnp.mean(values * values, axis=-1, keepdims=True)
        normed_ref[...] = (values * lax.rsqrt(mean_sq + EPS) * gain_ref[...]).astype(BF16)
        fetch_qkv.wait()
        put_qkv(normed_ref[...], qkv_buf, out_refs, full_ref, book)
        put.wait()

    return pl.pallas_call(
        body,
        in_specs=[SM, ANY, VM, VM, VM, VM, ANY, ANY] + [VM] * (books + 8),
        out_specs=[ANY] + [VM] * (2 + books),
        out_shape=[jax.ShapeDtypeStruct((rows, width), BF16)]
        + [jax.ShapeDtypeStruct((rows, deep), BF16)] * 2
        + [jax.ShapeDtypeStruct((share, 3 * part), BF16)] * books,
        input_output_aliases={1: 0},
        scratch_shapes=[
            pltpu.VMEM((rows, books * cols), BF16),
            pltpu.VMEM((cols, 2 * block), BF16),
            pltpu.VMEM((3, deep, part), BF16),
            pltpu.VMEM((rows, 3 * part), F32),
            pltpu.VMEM((rows, 2 * block), BF16),
            pltpu.SemaphoreType.DMA((3,)),
        ],
        compiler_params=pltpu.CompilerParams(vmem_limit_bytes=LATE_LIMIT),
        cost_estimate=cost(
            rows * width * (books * cols + deep) // 2 + 6 * rows * deep * part,
            width * (books * cols + deep) // 2 + 6 * deep * part,
        ),
    )(
        place,
        early,
        acc,
        hidden,
        entry,
        gain,
        own,
        weights,
        *mixed,
        *[out_pieces[i] for i in used],
        *[in_pieces[i] for i in used],
    )


def qkv_kernel(place, normed, weights, books, part, chunks):
    rows, deep = normed.shape
    cols = deep // chunks
    block = rows // books

    def body(place_ref, normed_ref, qkv_ref, *refs):
        put_qkv(normed_ref[...], qkv_ref, refs[:books], refs[books], place_ref[1])

    return pl.pallas_call(
        body,
        grid=(1,),
        in_specs=[
            SM,
            pl.BlockSpec((rows, deep), lambda i: (0, 0)),
            pl.BlockSpec((3, deep, cols), lambda i: (0, 0, part)),
        ],
        out_specs=[pl.BlockSpec((block, 3 * cols), lambda i: (0, 0))] * books,
        out_shape=[jax.ShapeDtypeStruct((block, 3 * cols), BF16)] * books,
        scratch_shapes=[pltpu.VMEM((rows, 3 * cols), F32)],
        compiler_params=PARAMS,
        cost_estimate=cost(6 * rows * deep * cols, 6 * deep * cols),
    )(place, normed, weights)


def two(values):
    high = values.astype(BF16)
    return high, (values - high.astype(F32)).astype(BF16)


def depth_attention(place, arrived):
    books = len(arrived)
    rows, wide = arrived[0].shape
    cols = wide // 3
    scale = 1.0 / (DHD**0.5)

    def body(place_ref, *refs):
        arrived_refs = refs[:books]
        out_refs = refs[books : 2 * books]
        all_ref, result_ref = refs[2 * books :]
        book = place_ref[1]
        for at in range(books):
            all_ref[lax.rem(book + books - at, books)] = arrived_refs[at][...]
        lane = lax.broadcasted_iota(jnp.int32, (cols, 128), 0) // DHD
        head = lax.broadcasted_iota(jnp.int32, (cols, 128), 1)
        gather = (lane == head).astype(BF16)
        lane_t = lax.broadcasted_iota(jnp.int32, (128, cols), 1) // DHD
        head_t = lax.broadcasted_iota(jnp.int32, (128, cols), 0)
        scatter = (lane_t == head_t).astype(BF16)
        for c in range(books):
            query = all_ref[c, :, :cols].astype(F32)
            scores = []
            for j in range(c + 1):
                high, low = two(query * all_ref[j, :, cols : 2 * cols].astype(F32))
                scores.append((dot(high, gather) + dot(low, gather)) * scale)
            highest = functools.reduce(jnp.maximum, scores)
            weights = [jnp.exp(score - highest) for score in scores]
            inverse = 1.0 / functools.reduce(jnp.add, weights)
            mixed = jnp.zeros((rows, cols), F32)
            for j in range(c + 1):
                mixed += dot(weights[j].astype(BF16), scatter) * all_ref[j, :, 2 * cols :].astype(F32)
            high, low = two(inverse)
            mixed = mixed * (dot(high, scatter) + dot(low, scatter))
            result_ref[c] = mixed.astype(BF16)
        for at in range(books):
            out_refs[at][...] = result_ref[lax.rem(book + at, books)]

    return pl.pallas_call(
        body,
        in_specs=[SM] + [VM] * books,
        out_specs=[VM] * books,
        out_shape=[jax.ShapeDtypeStruct((rows, cols), BF16)] * books,
        scratch_shapes=[pltpu.VMEM((books, rows, wide), BF16), pltpu.VMEM((books, rows, cols), BF16)],
        compiler_params=PARAMS,
        cost_estimate=cost(4 * books * books * rows * cols * 128, 8 * books * rows * cols),
    )(place, *arrived)


def depth_output(place, stream, returned, weight):
    rows, deep = stream.shape
    chunks = len(returned)
    books = len(returned[0])
    block = rows // books
    cols = deep // chunks
    flat = [value for part in returned for value in part]

    def body(place_ref, stream_ref, weight_ref, *refs):
        parts = refs[: chunks * books]
        out_ref, cat_ref = refs[chunks * books :]
        book = place_ref[1]
        for k in range(chunks):
            for at in range(books):
                row = pl.multiple_of(lax.rem(book + books - at, books) * block, block)
                cat_ref[pl.ds(row, block), k * cols : (k + 1) * cols] = parts[k * books + at][...]
        result = dot(cat_ref[...], weight_ref[...]) + stream_ref[...].astype(F32)
        out_ref[...] = result.astype(BF16)

    return pl.pallas_call(
        body,
        in_specs=[SM] + [VM] * (2 + chunks * books),
        out_specs=VM,
        out_shape=jax.ShapeDtypeStruct((rows, deep), BF16),
        scratch_shapes=[pltpu.VMEM((rows, deep), BF16)],
        compiler_params=PARAMS,
        cost_estimate=cost(2 * rows * deep * deep, 2 * deep * deep),
    )(place, stream, weight, *flat)


def shards(
    hidden,
    temporal_gain,
    temporal_qkv,
    temporal_out,
    codebook_ids,
    embedding,
    input_weight,
    depth_gain,
    depth_qkv,
    depth_out,
):
    seqs, frames, width = hidden.shape
    rows = seqs * frames
    deep = depth_gain.shape[1]
    cols = temporal_out.shape[0]
    size = lax.axis_size("seq")
    books = lax.axis_size("cb")

    place = jnp.stack([lax.axis_index("seq"), lax.axis_index("cb")]).astype(jnp.int32)
    block = width // size
    ring = [lax.dynamic_slice_in_dim(temporal_out, lax.axis_index("seq") * block, block, 1)]
    for _ in range(1, books):
        ring.append(shift(ring[-1], "cb", 1))
    half = input_weight.shape[1] // 2
    in_pieces = spread_halves(input_weight[0, :half], input_weight[0, half:], "seq")
    half = cols // 2
    first = jnp.stack([piece[:half] for piece in ring[1:]])
    second = jnp.stack([piece[half:] for piece in ring[1:]])
    out_pieces = spread_halves(first, second, "seq")

    entry = jnp.take(embedding[0], codebook_ids.reshape(rows), axis=0)

    packed = project(hidden, temporal_gain, temporal_qkv)
    own_mixed = temporal_attention(packed)
    mixed = [own_mixed] + [shift(own_mixed, "cb", by) for by in range(1, books)]
    late = size - 2
    flat = hidden.reshape(rows, width)
    early, acc = early_output(place, flat, mixed, temporal_out, out_pieces, in_pieces, late)
    temporal, stream, normed, *sent = late_output(
        place, early, acc, flat, mixed, temporal_out, out_pieces, in_pieces,
        entry, depth_gain, depth_qkv[0], late, CHUNKS,
    )
    arrived, returned = [], []
    for part in range(CHUNKS):
        if part > 0:
            sent = qkv_kernel(place, normed, depth_qkv[0], books, part, CHUNKS)
        arrived.append([sent[0]] + [shift(sent[by], "cb", by) for by in range(1, books)])
    for part in range(CHUNKS):
        result = depth_attention(place, arrived[part])
        returned.append([result[0]] + [shift(result[by], "cb", by) for by in range(1, books)])
    depth = depth_output(place, stream, returned, depth_out[0])
    return (temporal.reshape(seqs, frames, width), depth.reshape(seqs, frames, 1, deep))


def solution(mesh):
    placed = (
        P(None, "seq", None),
        P(),
        P(None, None, "cb"),
        P("cb", None),
        P(None, "seq", "cb"),
        P("cb", None, None),
        P("cb", "seq", None),
        P("cb", None),
        P("cb", None, None, None),
        P("cb", None, None),
    )
    return jax.shard_map(
        shards,
        mesh=mesh,
        in_specs=placed,
        out_specs=(P(None, "seq", None), P(None, "seq", "cb", None)),
        check_vma=False,
    )
```

```python
import functools

import jax
import jax.numpy as jnp
from jax import lax
from jax.experimental import pallas as pl
from jax.experimental.pallas import tpu as pltpu
from jax.sharding import PartitionSpec as P


HD = 128
DHD = 64
EPS = 1e-05
NEG = -1e30
F32 = jnp.float32
BF16 = jnp.bfloat16
CHUNKS = 2
MIB = 1024 * 1024


VM = pl.BlockSpec(memory_space=pltpu.VMEM)
SM = pl.BlockSpec(memory_space=pltpu.SMEM)
ANY = pl.BlockSpec(memory_space=pl.ANY)


def limit(mib):
    return pltpu.CompilerParams(vmem_limit_bytes=mib * MIB)


def cost(flops, moved):
    return pl.CostEstimate(flops=flops, bytes_accessed=moved, transcendentals=0)


def dot(a, b):
    return jnp.dot(a, b, preferred_element_type=F32)


def flip(x, axis, bit):
    return lax.ppermute(x, axis, [(i, i ^ bit) for i in range(lax.axis_size(axis))])


def shift(x, axis, by):
    size = lax.axis_size(axis)
    return lax.ppermute(x, axis, [(i, (i + by) % size) for i in range(size)])


def ici_bits(size):
    return [1 << place for place in range(1, size.bit_length() - 1)]


def spread(piece, axis, order, trim):
    held = {0: piece}
    far = sum(order)
    for bit in order:
        found = {}
        for at, value in held.items():
            to = at ^ bit
            found[to] = flip(trim(value) if to == far else value, axis, bit)
        held.update(found)
    held.update({at ^ 1: flip(v, axis, 1) for at, v in list(held.items())})
    return held


def spread_halves(first, second, axis, trim=lambda value: value):
    size = lax.axis_size(axis)
    a = spread(first, axis, ici_bits(size), trim)
    b = spread(second, axis, ici_bits(size)[::-1], trim)
    return [half for at in range(size) for half in (a[at], b[at])]


def direct_steps(books):
    return [1, books - 1] if books > 3 else []


def project_body(hidden_ref, gain_ref, weight_ref, out_ref, normed_ref):
    seqs, heads, frames, _ = out_ref.shape
    rows = normed_ref.shape[0]
    step = min(64, rows)

    @pl.when(pl.program_id(0) == 0)
    def _():
        def one(at, carry):
            span = pl.ds(pl.multiple_of(at * step, step), step)
            values = hidden_ref[span, :].astype(F32)
            mean_sq = jnp.mean(values * values, axis=-1, keepdims=True)
            normed_ref[span, :] = (values * lax.rsqrt(mean_sq + EPS) * gain_ref[...]).astype(BF16)
            return carry

        lax.fori_loop(0, rows // step, one, 0)

    result = dot(normed_ref[...], weight_ref[0]).astype(BF16)
    for s in range(seqs):
        for h in range(heads):
            out_ref[s, h] = result[s * frames : (s + 1) * frames, h * HD : (h + 1) * HD]


def project(hidden, gain, weight):
    seqs, frames, width = hidden.shape
    cols = weight.shape[2]
    heads = cols // HD
    per = min(2, heads)
    parts = heads // per
    rows = seqs * frames
    return pl.pallas_call(
        project_body,
        grid=(3 * parts,),
        in_specs=[
            pl.BlockSpec((rows, width), lambda i: (0, 0)),
            pl.BlockSpec((1, width), lambda i: (0, 0)),
            pl.BlockSpec((1, width, per * HD), lambda i: (i // parts, 0, i % parts)),
        ],
        out_specs=pl.BlockSpec((seqs, per, frames, HD), lambda i: (0, i % parts, 0, i // parts)),
        out_shape=jax.ShapeDtypeStruct((seqs, heads, frames, 3 * HD), BF16),
        scratch_shapes=[pltpu.VMEM((rows, width), BF16)],
        compiler_params=limit(58),
        cost_estimate=cost(6 * rows * width * cols, 6 * width * cols + 2 * rows * width),
    )(hidden.reshape(rows, width), gain.reshape(1, width), weight)


def attend_body(packed_ref, out_ref):
    length = packed_ref.shape[0]
    block = min(256, length)
    scale = 1.0 / (HD**0.5)
    for start in range(0, length, block):
        stop = start + block
        scores = (
            lax.dot_general(
                packed_ref[start:stop, :HD],
                packed_ref[:stop, HD : 2 * HD],
                (((1,), (1,)), ((), ())),
                preferred_element_type=F32,
            )
            * scale
        )
        rows = lax.broadcasted_iota(jnp.int32, scores.shape, 0) + start
        cols = lax.broadcasted_iota(jnp.int32, scores.shape, 1)
        scores = jnp.where(cols <= rows, scores, NEG)
        weights = jnp.exp(scores - jnp.max(scores, axis=-1, keepdims=True))
        totals = jnp.sum(weights, axis=-1, keepdims=True)
        mixed = dot(weights.astype(BF16), packed_ref[:stop, 2 * HD :])
        out_ref[start:stop, :] = (mixed / totals).astype(BF16)


def attend_pair(packed):
    length = packed.shape[0]
    return pl.pallas_call(
        attend_body,
        in_specs=[VM],
        out_specs=VM,
        out_shape=jax.ShapeDtypeStruct((length, HD), BF16),
        compiler_params=limit(20),
        cost_estimate=cost(3 * length * length * HD, 8 * length * HD),
    )(packed)


def temporal_attention(packed):
    seqs, heads, frames, _ = packed.shape
    pairs = seqs * heads
    size = lax.axis_size("seq")
    if pairs == size:
        whole = lax.all_to_all(packed.reshape(pairs, frames, 3 * HD), "seq", split_axis=0, concat_axis=0, tiled=True)
        mixed = attend_pair(whole.reshape(size * frames, 3 * HD))
        return lax.all_to_all(
            mixed.reshape(size, frames, HD), "seq", split_axis=0, concat_axis=0, tiled=True
        )
    queries = packed[..., :HD]
    both = lax.all_gather(packed[..., HD:], "seq", axis=2, tiled=True)
    keys, values = both[..., :HD], both[..., HD:]
    scores = jnp.einsum("shqd,shkd->shqk", queries, keys, preferred_element_type=F32) / (HD**0.5)
    at = lax.axis_index("seq") * frames + jnp.arange(frames, dtype=jnp.int32)
    allowed = jnp.arange(size * frames, dtype=jnp.int32)[None, :] <= at[:, None]
    scores = jnp.where(allowed, scores, NEG)
    weights = jnp.exp(scores - jnp.max(scores, axis=-1, keepdims=True))
    totals = jnp.sum(weights, axis=-1, keepdims=True)
    mixed = jnp.einsum(
        "shqk,shkd->shqd", weights.astype(BF16), values, preferred_element_type=F32
    )
    return (mixed / totals).astype(BF16).reshape(pairs, frames, HD)


def put_mixed(mixed_refs, cat_ref):
    pairs, frames, _ = mixed_refs[0].shape
    cols = cat_ref.shape[1] // len(mixed_refs)
    heads = cols // HD
    for group, ref in enumerate(mixed_refs):
        for pair in range(pairs):
            s, h = pair // heads, pair % heads
            at = group * cols + h * HD
            cat_ref[s * frames : (s + 1) * frames, at : at + HD] = ref[pair]


def chip_start(me, at, wide):
    return pl.multiple_of(lax.shift_right_logical(me ^ at, 1) * wide, wide)


def early_output(place, hidden, mixed, own, out_pieces, in_pieces, late):
    rows, width = hidden.shape
    cols = own.shape[0]
    groups = len(mixed)
    size = len(out_pieces) // 2
    block = width // size
    half, deep = in_pieces[0].shape
    chips = [at for at in range(0, size, 2) if at != late]
    count = len(chips)
    used = [2 * (at + core) + side for at in chips for core in range(2) for side in range(2)]

    def body(place_ref, hidden_ref, *refs):
        mixed_refs = refs[:groups]
        own_ref = refs[groups]
        outs = refs[groups + 1 : groups + 1 + 4 * count]
        ins = refs[groups + 1 + 4 * count : groups + 1 + 8 * count]
        out_ref, acc_ref, cat_ref, out_buf, in_buf, out_sems, in_sems = refs[groups + 1 + 8 * count :]
        me = place_ref[0]

        def out_copies(index):
            at = chips[index // 2] + index % 2
            column = pl.multiple_of((me ^ at) * block, block)
            found = []
            for side in range(2):
                found.append(
                    pltpu.make_async_copy(
                        own_ref.at[side * (cols // 2) : (side + 1) * (cols // 2), pl.ds(column, block)],
                        out_buf.at[index, 0, side],
                        out_sems.at[index, side],
                    )
                )
                found.append(
                    pltpu.make_async_copy(
                        outs[2 * index + side], out_buf.at[index, 1:, side], out_sems.at[index, 2 + side]
                    )
                )
            return found

        def in_copies(chip):
            found = []
            for core in range(2):
                where = (me ^ core) & 1
                for side in range(2):
                    found.append(
                        pltpu.make_async_copy(
                            ins[4 * chip + 2 * core + side],
                            in_buf.at[chip, where, side],
                            in_sems.at[chip, 2 * core + side],
                        )
                    )
            return found

        for index in range(2 * count):
            for copy in out_copies(index):
                copy.start()
        for chip in range(count):
            for copy in in_copies(chip):
                copy.start()
        put_mixed(mixed_refs, cat_ref)
        for index in range(2 * count):
            at = chips[index // 2] + index % 2
            for copy in out_copies(index):
                copy.wait()
            span = pl.ds(pl.multiple_of((me ^ at) * block, block), block)
            summed = dot(cat_ref[...], out_buf[index].reshape(groups * cols, block))
            out_ref[:, span] = (hidden_ref[:, span].astype(F32) + summed).astype(BF16)
        for chip in range(count):
            for copy in in_copies(chip):
                copy.wait()
            span = pl.ds(chip_start(me, chips[chip], 4 * half), 4 * half)
            term = dot(out_ref[:, span], in_buf[chip].reshape(4 * half, deep))
            if chip == 0:
                acc_ref[...] = term
            else:
                acc_ref[...] += term

    return pl.pallas_call(
        body,
        in_specs=[SM, VM] + [VM] * groups + [ANY] * (1 + 8 * count),
        out_specs=[VM, VM],
        out_shape=[
            jax.ShapeDtypeStruct((rows, width), BF16),
            jax.ShapeDtypeStruct((rows, deep), F32),
        ],
        scratch_shapes=[
            pltpu.VMEM((rows, groups * cols), BF16),
            pltpu.VMEM((2 * count, groups, 2, cols // 2, block), BF16),
            pltpu.VMEM((count, 2, 2, half, deep), BF16),
            pltpu.SemaphoreType.DMA((2 * count, 4)),
            pltpu.SemaphoreType.DMA((count, 4)),
        ],
        compiler_params=limit(30),
        cost_estimate=cost(
            2 * rows * width * (groups * cols + deep), 2 * width * (groups * cols + deep)
        ),
    )(
        place,
        hidden,
        *mixed,
        own,
        *[out_pieces[i] for i in used],
        *[in_pieces[i] for i in used],
    )


def put_qkv(normed, weights, part, out_refs, full_ref, book):
    books = len(out_refs)
    block, wide = out_refs[0].shape
    cols = wide // 3
    for which in range(3):
        weight = weights[which, :, part * cols : (part + 1) * cols]
        full_ref[:, which * cols : (which + 1) * cols] = dot(normed, weight)
    for at in range(books):
        row = pl.multiple_of(lax.rem(book + at, books) * block, block)
        out_refs[at][...] = full_ref[pl.ds(row, block), :].astype(BF16)


def late_output(
    place, early, acc, hidden, mixed, own, out_pieces, direct, in_pieces, entry, gain, weights, late, chunks
):
    rows, width = hidden.shape
    books = len(mixed)
    size = len(out_pieces) // 2
    cols = own.shape[0]
    block = width // size
    half, deep = in_pieces[0].shape
    part = deep // chunks
    share = rows // books
    used = [2 * (late + core) + side for core in range(2) for side in range(2)]
    steps = sorted(direct)
    first = 2 if steps else 1
    count = out_pieces[used[0]].shape[0]
    fars = [direct[step][core].reshape(2, cols // 2, block) for core in range(2) for step in steps]

    def body(place_ref, _, acc_ref, hidden_ref, entry_ref, gain_ref, own_ref, qkv_ref, *refs):
        mixed_refs, refs = refs[:books], refs[books:]
        ins, refs = refs[:4], refs[4:]
        outs, refs = refs[:4], refs[4:]
        far_refs, refs = refs[: len(fars)], refs[len(fars) :]
        out_ref, stream_ref, normed_ref = refs[:3]
        out_refs = refs[3 : 3 + books]
        cat_ref, out_buf, full_ref, old_buf, new_buf, sems, ends = refs[3 + books :]
        me = place_ref[0]
        book = place_ref[1]
        start = chip_start(me, late, 2 * block)

        def copies(core):
            column = pl.multiple_of((me ^ (late + core)) * block, block)
            found = []
            for side in range(2):
                found.append(
                    pltpu.make_async_copy(
                        own_ref.at[side * (cols // 2) : (side + 1) * (cols // 2), pl.ds(column, block)],
                        out_buf.at[core, 0, side],
                        sems.at[core, side],
                    )
                )
                found.append(
                    pltpu.make_async_copy(
                        outs[2 * core + side],
                        out_buf.at[core, first : first + count, side],
                        sems.at[core, 2 + side],
                    )
                )
            for index, step in enumerate(steps):
                found.append(
                    pltpu.make_async_copy(
                        far_refs[core * len(steps) + index],
                        out_buf.at[core, step],
                        sems.at[core, 4 + index],
                    )
                )
            return found

        old = pltpu.make_async_copy(hidden_ref.at[:, pl.ds(start, 2 * block)], old_buf, ends.at[0])
        for core in range(2):
            for copy in copies(core):
                copy.start()
        old.start()
        put_mixed(mixed_refs, cat_ref)
        total = acc_ref[...] + entry_ref[...].astype(F32)
        for core in range(2):
            local = pl.ds(pl.multiple_of(((me ^ core) & 1) * block, block), block)
            for copy in copies(core):
                copy.wait()
            if core == 0:
                old.wait()
            summed = dot(cat_ref[...], out_buf[core].reshape(books * cols, block))
            value = (old_buf[:, local].astype(F32) + summed).astype(BF16)
            new_buf[:, local] = value
            for side in range(2):
                total += dot(value[:, side * half : (side + 1) * half], ins[2 * core + side][...])
        put = pltpu.make_async_copy(new_buf, out_ref.at[:, pl.ds(start, 2 * block)], ends.at[1])
        put.start()
        stream = total.astype(BF16)
        stream_ref[...] = stream
        values = stream.astype(F32)
        mean_sq = jnp.mean(values * values, axis=-1, keepdims=True)
        normed_ref[...] = (values * lax.rsqrt(mean_sq + EPS) * gain_ref[...]).astype(BF16)
        put_qkv(normed_ref[...], qkv_ref, 0, out_refs, full_ref, book)
        put.wait()

    return pl.pallas_call(
        body,
        in_specs=[SM, ANY, VM, ANY, VM, VM, ANY, VM] + [VM] * (books + 4) + [ANY] * (4 + len(fars)),
        out_specs=[ANY] + [VM] * (2 + books),
        out_shape=[jax.ShapeDtypeStruct((rows, width), BF16)]
        + [jax.ShapeDtypeStruct((rows, deep), BF16)] * 2
        + [jax.ShapeDtypeStruct((share, 3 * part), BF16)] * books,
        input_output_aliases={1: 0},
        scratch_shapes=[
            pltpu.VMEM((rows, books * cols), BF16),
            pltpu.VMEM((2, books, 2, cols // 2, block), BF16),
            pltpu.VMEM((rows, 3 * part), F32),
            pltpu.VMEM((rows, 2 * block), BF16),
            pltpu.VMEM((rows, 2 * block), BF16),
            pltpu.SemaphoreType.DMA((2, 4 + len(steps))),
            pltpu.SemaphoreType.DMA((2,)),
        ],
        compiler_params=limit(20),
        cost_estimate=cost(
            rows * width * (books * cols + deep) // 2 + 6 * rows * deep * part,
            width * (books * cols + deep) // 2 + 6 * deep * part,
        ),
    )(
        place,
        early,
        acc,
        hidden,
        entry,
        gain,
        own,
        weights,
        *mixed,
        *[in_pieces[i] for i in used],
        *[out_pieces[i] for i in used],
        *fars,
    )


def qkv_kernel(place, normed, weights, books, part, chunks):
    rows, deep = normed.shape
    cols = deep // chunks
    block = rows // books

    def body(place_ref, normed_ref, qkv_ref, *refs):
        put_qkv(normed_ref[...], qkv_ref, part, refs[:books], refs[books], place_ref[1])

    return pl.pallas_call(
        body,
        in_specs=[SM, VM, VM],
        out_specs=[VM] * books,
        out_shape=[jax.ShapeDtypeStruct((block, 3 * cols), BF16)] * books,
        scratch_shapes=[pltpu.VMEM((rows, 3 * cols), F32)],
        compiler_params=limit(20),
        cost_estimate=cost(6 * rows * deep * cols, 6 * deep * cols),
    )(place, normed, weights)


def two(values):
    high = values.astype(BF16)
    return high, (values - high.astype(F32)).astype(BF16)


def depth_attention(place, arrived):
    books = len(arrived)
    rows, wide = arrived[0].shape
    cols = wide // 3
    scale = 1.0 / (DHD**0.5)

    def body(place_ref, *refs):
        arrived_refs = refs[:books]
        out_refs = refs[books : 2 * books]
        all_ref, result_ref = refs[2 * books :]
        book = place_ref[1]
        for at in range(books):
            all_ref[lax.rem(book + books - at, books)] = arrived_refs[at][...]
        lane = lax.broadcasted_iota(jnp.int32, (cols, 128), 0) // DHD
        head = lax.broadcasted_iota(jnp.int32, (cols, 128), 1)
        gather = (lane == head).astype(BF16)
        lane_t = lax.broadcasted_iota(jnp.int32, (128, cols), 1) // DHD
        head_t = lax.broadcasted_iota(jnp.int32, (128, cols), 0)
        scatter = (lane_t == head_t).astype(BF16)
        for c in range(books):
            query = all_ref[c, :, :cols].astype(F32)
            scores = []
            for j in range(c + 1):
                high, low = two(query * all_ref[j, :, cols : 2 * cols].astype(F32))
                scores.append((dot(high, gather) + dot(low, gather)) * scale)
            highest = functools.reduce(jnp.maximum, scores)
            weights = [jnp.exp(score - highest) for score in scores]
            inverse = 1.0 / functools.reduce(jnp.add, weights)
            mixed = jnp.zeros((rows, cols), F32)
            for j in range(c + 1):
                mixed += dot(weights[j].astype(BF16), scatter) * all_ref[j, :, 2 * cols :].astype(F32)
            high, low = two(inverse)
            mixed = mixed * (dot(high, scatter) + dot(low, scatter))
            result_ref[c] = mixed.astype(BF16)
        for at in range(books):
            out_refs[at][...] = result_ref[lax.rem(book + at, books)]

    return pl.pallas_call(
        body,
        in_specs=[SM] + [VM] * books,
        out_specs=[VM] * books,
        out_shape=[jax.ShapeDtypeStruct((rows, cols), BF16)] * books,
        scratch_shapes=[pltpu.VMEM((books, rows, wide), BF16), pltpu.VMEM((books, rows, cols), BF16)],
        compiler_params=limit(20),
        cost_estimate=cost(4 * books * books * rows * cols * 128, 8 * books * rows * cols),
    )(place, *arrived)


def depth_output(place, stream, returned, weight):
    rows, deep = stream.shape
    chunks = len(returned)
    books = len(returned[0])
    block = rows // books
    cols = deep // chunks
    flat = [value for part in returned for value in part]

    def body(place_ref, stream_ref, weight_ref, *refs):
        parts = refs[: chunks * books]
        out_ref, cat_ref = refs[chunks * books :]
        book = place_ref[1]
        for k in range(chunks):
            for at in range(books):
                row = pl.multiple_of(lax.rem(book + books - at, books) * block, block)
                cat_ref[pl.ds(row, block), k * cols : (k + 1) * cols] = parts[k * books + at][...]
        result = dot(cat_ref[...], weight_ref[...]) + stream_ref[...].astype(F32)
        out_ref[...] = result.astype(BF16)

    return pl.pallas_call(
        body,
        in_specs=[SM] + [VM] * (2 + chunks * books),
        out_specs=VM,
        out_shape=jax.ShapeDtypeStruct((rows, deep), BF16),
        scratch_shapes=[pltpu.VMEM((rows, deep), BF16)],
        compiler_params=limit(20),
        cost_estimate=cost(2 * rows * deep * deep, 2 * deep * deep),
    )(place, stream, weight, *flat)


def shards(
    hidden,
    temporal_gain,
    temporal_qkv,
    temporal_out,
    codebook_ids,
    embedding,
    input_weight,
    depth_gain,
    depth_qkv,
    depth_out,
):
    seqs, frames, width = hidden.shape
    rows = seqs * frames
    deep = depth_gain.shape[1]
    cols = temporal_out.shape[0]
    size = lax.axis_size("seq")
    books = lax.axis_size("cb")

    place = jnp.stack([lax.axis_index("seq"), lax.axis_index("cb")]).astype(jnp.int32)
    block = width // size
    ring = [lax.dynamic_slice_in_dim(temporal_out, lax.axis_index("seq") * block, block, 1)]
    for _ in range(1, books):
        ring.append(shift(ring[-1], "cb", 1))
    half = input_weight.shape[1] // 2
    in_pieces = spread_halves(input_weight[0, :half], input_weight[0, half:], "seq")
    half = cols // 2
    first = jnp.stack([piece[:half] for piece in ring[1:]])
    second = jnp.stack([piece[half:] for piece in ring[1:]])
    steps = direct_steps(books)
    trim = (lambda value: value[1:-1]) if steps else (lambda value: value)
    out_pieces = spread_halves(first, second, "seq", trim)
    late = size - 2
    there = lax.dynamic_slice_in_dim(temporal_out, (lax.axis_index("seq") ^ late) * block, block, 1)
    direct = {}
    for step in steps:
        piece = shift(there, "cb", step)
        direct[step] = (piece, flip(piece, "seq", 1))

    entry = jnp.take(embedding[0], codebook_ids.reshape(rows), axis=0)

    packed = project(hidden, temporal_gain, temporal_qkv)
    own_mixed = temporal_attention(packed)
    mixed = [own_mixed] + [shift(own_mixed, "cb", by) for by in range(1, books)]
    flat = hidden.reshape(rows, width)
    early, acc = early_output(place, flat, mixed, temporal_out, out_pieces, in_pieces, late)
    temporal, stream, normed, *sent = late_output(
        place, early, acc, flat, mixed, temporal_out, out_pieces, direct, in_pieces,
        entry, depth_gain, depth_qkv[0], late, CHUNKS,
    )
    arrived, returned = [], []
    for part in range(CHUNKS):
        if part > 0:
            sent = qkv_kernel(place, normed, depth_qkv[0], books, part, CHUNKS)
        arrived.append([sent[0]] + [shift(sent[by], "cb", by) for by in range(1, books)])
    for part in range(CHUNKS):
        result = depth_attention(place, arrived[part])
        returned.append([result[0]] + [shift(result[by], "cb", by) for by in range(1, books)])
    depth = depth_output(place, stream, returned, depth_out[0])
    return (temporal.reshape(seqs, frames, width), depth.reshape(seqs, frames, 1, deep))


def solution(mesh):
    placed = (
        P(None, "seq", None),
        P(),
        P(None, None, "cb"),
        P("cb", None),
        P(None, "seq", "cb"),
        P("cb", None, None),
        P("cb", "seq", None),
        P("cb", None),
        P("cb", None, None, None),
        P("cb", None, None),
    )
    return jax.shard_map(
        shards,
        mesh=mesh,
        in_specs=placed,
        out_specs=(P(None, "seq", None), P(None, "seq", "cb", None)),
        check_vma=False,
    )
```
